512 devices in a mesh: ep: 128 (over y, z, core), dp: 4 (over x).
Axes of the slice: x: 4, y: 8, z: 8, core: 2. Of those that a mesh axis runs over, the one named last changes fastest.
Arguments:
- activations: float32 [256, 256, 768], P('ep', 'dp'), may hold values from -6 to 6
- out_grads: float32 [256, 256, 512], P('ep', 'dp'), may hold values from -6 to 6
- counts: int32 [256, 4], P('ep', 'dp'), may hold values from 1 to 64
- slot_weights: float32 [256, 768, 512], P('ep', None, 'dp'), may hold values from -0.21875 to 0.21875
- master: float32 [128, 768, 512], P(None, 'ep', 'dp'), may hold values from -0.21875 to 0.21875
- moment_one: float32 [128, 768, 512], P(None, 'ep', 'dp'), may hold values from -6 to 6
- moment_two: float32 [128, 768, 512], P(None, 'ep', 'dp'), may hold values from 1 to 100
- old_table: int32 [256, 1], replicated, may hold values from 0 to 127
- new_table: int32 [256, 1], replicated, may hold values from 0 to 127
Outputs:
- outputs: float32 [256, 256, 512], P('ep', 'dp')
- input_grads: float32 [256, 256, 768], P('ep', 'dp')
- new_master: float32 [128, 768, 512], P(None, 'ep', 'dp')
- new_moment_one: float32 [128, 768, 512], P(None, 'ep', 'dp')
- new_moment_two: float32 [128, 768, 512], P(None, 'ep', 'dp')
- new_slots: float32 [256, 768, 512], P('ep', None, 'dp')
The draws below stay inside these ranges and needn't reach their ends.
Inputs may be any that keep to these rules, and one draw needn't show every extreme that they name: `old_table`: every expert is named by at least one old slot. `new_table`: every expert is named by at least one new slot.
All inputs are finite; a program needn't handle non-finite values.
Results may differ from the reference program's by a relative error of at most 0.00007.
Values sent between devices are 32-bit elements; how exact they have to be, the bound alone decides.
No kernel may reach another device: no remote copies, remote signals or barrier semaphores. Data moves between devices by JAX's collectives and lax.ppermute only.
A program may use at most 64 MiB of HBM per device.

```python
import math
import jax
import jax.numpy as jnp
from jax import lax

FF = 768
DS = 512
ROWS = 64
STEP = 100
EXPERTS = 128
SLOTS = 256
TOKS = 256
N_DP = 4


def set_ends(values, own_key, low, top_value):
    longest = values.shape.index(max(values.shape))
    spots = []
    for shift in (0, 1):
        where = [jax.random.randint(jax.random.fold_in(own_key, axis), (), 0, length) for axis, length in enumerate(values.shape)]
        where[longest] = (where[longest] + shift) % values.shape[longest]
        spots.append(tuple(where))
    return values.at[spots[0]].set(low).at[spots[1]].set(top_value)


def block_levels(key, extent, pieces, low, top_value):
    gain = 1.0
    for axis_at, parts in pieces:
        steps = jax.random.uniform(jax.random.fold_in(jax.random.fold_in(key, 6), axis_at), (parts,), jnp.float32, low / len(pieces), top_value / len(pieces))
        gain = gain * jnp.repeat(jnp.exp(steps), extent[axis_at] // parts).reshape((-1,) + (1,) * (len(extent) - 1 - axis_at))
    return gain


def choose_distinct(stream_key, rows, amount, top, lift):
    sequence = jax.random.permutation(jax.random.fold_in(stream_key, 1), amount)
    boost = sequence
    for power in range(3):
        boost = boost * boost // amount
    boost = boost * lift // amount
    tickets = jax.random.randint(jax.random.fold_in(stream_key, 2), (rows, amount), 0, 4096) + boost
    fixed_rows = jax.random.permutation(jax.random.fold_in(stream_key, 3), rows)[jnp.arange(amount) % rows]
    tickets = jnp.where(jnp.arange(rows)[:, None] == fixed_rows[None, :], 1 << 14, tickets)
    merit = tickets * amount + jnp.arange(amount)
    return lax.top_k(merit.astype(jnp.int32), top)[1].astype(jnp.int32)


def normal_values(own_key, extent, width, most, pieces=(), kind=jnp.bfloat16):
    factor_of = block_levels(own_key, extent, pieces, -0.22, 0.18) if pieces else 1.0
    array = jax.random.normal(own_key, extent, jnp.float32) * width * factor_of
    return jnp.minimum(jnp.maximum(array, -most), most).astype(kind)


def setup_inputs(seed: int = 0) -> dict:
    key_of = jax.random.split(jax.random.key(seed), 10)
    activations = normal_values(key_of[0], (SLOTS, TOKS, FF), 1.0, 6.0, ((0, 128), (1, 4)), jnp.float32)
    out_grads = normal_values(key_of[1], (SLOTS, TOKS, DS), 1.0, 6.0, ((0, 128), (1, 4)), jnp.float32)
    counts = set_ends(jax.random.randint(key_of[2], (SLOTS, N_DP), 1, ROWS + 1), jax.random.fold_in(key_of[2], 1), 1, ROWS).astype(jnp.int32)
    slot_weights = normal_values(key_of[3], (SLOTS, FF, DS), FF ** -0.5, 0.21875, ((0, 128), (2, 4)), jnp.float32)
    master = normal_values(key_of[4], (EXPERTS, FF, DS), FF ** -0.5, 0.21875, ((1, 128), (2, 4)), jnp.float32)
    moment_one = normal_values(key_of[5], (EXPERTS, FF, DS), 1.0, 6.0, ((1, 128), (2, 4)), jnp.float32)
    moment_two = jnp.clip(jnp.exp(math.log(100.0) - 4.6051702 * jax.random.uniform(key_of[6], (EXPERTS, FF, DS), jnp.float32) ** block_levels(key_of[6], (EXPERTS, FF, DS), ((1, 128), (2, 4)), -0.2, 0.2)), 1.0, 100.0)
    old_table = choose_distinct(key_of[7], SLOTS, EXPERTS, 1, 128)
    new_table = choose_distinct(key_of[8], SLOTS, EXPERTS, 1, 64)
    return {"activations": activations, "out_grads": out_grads, "counts": counts, "slot_weights": slot_weights, "master": master, "moment_one": moment_one, "moment_two": moment_two, "old_table": old_table, "new_table": new_table}


beta_one = 0.9
beta_two = 0.999
learn_rate = 0.02
epsilon = 1e-08
decay_rate = 0.1

def adamw(master, moment_one, moment_two, expert_grad):
    first_new = beta_one * moment_one + (1.0 - beta_one) * expert_grad
    second_new = beta_two * moment_two + (1.0 - beta_two) * expert_grad * expert_grad
    first_hat = first_new / (1.0 - beta_one ** STEP)
    second_hat = second_new / (1.0 - beta_two ** STEP)
    updated = master - learn_rate * (first_hat / (jnp.sqrt(second_hat) + epsilon) + decay_rate * master)
    return (updated, first_new, second_new)

def reference(activations, out_grads, counts, slot_weights, master, moment_one, moment_two, old_table, new_table):
    precise = lax.Precision.HIGHEST
    positions = jnp.arange(activations.shape[1], dtype=jnp.int32)
    limits = jnp.repeat(counts, ROWS, axis=1)
    live_rows = ((positions % ROWS)[None, :] < limits).astype(jnp.float32)
    masked_acts = activations * live_rows[:, :, None]
    masked_grads = out_grads * live_rows[:, :, None]
    outputs = jnp.einsum('srf,sfd->srd', masked_acts, slot_weights, precision=precise)
    input_grads = jnp.einsum('srd,sfd->srf', masked_grads, slot_weights, precision=precise)
    slot_grad = jnp.einsum('srf,srd->sfd', masked_acts, masked_grads, precision=precise)
    experts_ids = jnp.arange(EXPERTS, dtype=jnp.int32)
    old_onehot = (old_table[:, 0][None, :] == experts_ids[:, None]).astype(jnp.float32)
    expert_grad = jnp.einsum('es,sfd->efd', old_onehot, slot_grad, precision=precise)
    new_master, new_moment_one, new_moment_two = adamw(master, moment_one, moment_two, expert_grad)
    new_onehot = (new_table[:, 0][:, None] == experts_ids[None, :]).astype(jnp.float32)
    new_slots = jnp.einsum('se,efd->sfd', new_onehot, new_master, precision=precise)
    return (outputs, input_grads, new_master, new_moment_one, new_moment_two, new_slots)
```

```python
import jax
import jax.numpy as jnp
from jax import lax
from jax.experimental import pallas as pl
from jax.experimental.pallas import tpu as pltpu
from jax.sharding import PartitionSpec as P

STEP = 100


beta_one = 0.9
beta_two = 0.999
learn_rate = 0.02
epsilon = 1e-08
decay_rate = 0.1

LANES = 128


def halves(x):
    high = x.astype(jnp.bfloat16)
    low = (x - high.astype(jnp.float32)).astype(jnp.bfloat16)
    return high, low


def thirds(x):
    high = x.astype(jnp.bfloat16)
    rest = x - high.astype(jnp.float32)
    middle = rest.astype(jnp.bfloat16)
    low = (rest - middle.astype(jnp.float32)).astype(jnp.bfloat16)
    return high, middle, low


def dot(a, b, dims):
    return lax.dot_general(a, b, (dims, ((), ())), preferred_element_type=jnp.float32)


def dot_split(a, b, dims):
    (ah, al), (bh, bl) = a, b
    return dot(ah, bh, dims) + (dot(ah, bl, dims) + dot(al, bh, dims))


def grad_kernel(*refs):
    n = (len(refs) - 1) // 2
    acts, grads, out = refs[:n], refs[n : 2 * n], refs[-1]
    slots, _, ff = acts[0].shape
    for s in range(slots):
        a = jnp.concatenate([r[s] for r in acts], axis=0)
        g = jnp.concatenate([r[s] for r in grads], axis=0)
        out[pl.ds(s, ff, stride=slots), :] = dot_split(halves(a), halves(g), ((0,), (0,)))


def adamw_kernel(arrived, old_table, new_table, master, moment_one, moment_two,
                 new_master, new_one, new_two, send):
    rows, experts, _ = master.shape
    slots, owners = old_table.shape
    step = rows * slots
    ids = lax.broadcasted_iota(jnp.int32, (experts, owners), 0)

    def onehot(table):
        return jnp.concatenate(
            [(ids == table[p : p + 1, :]).astype(jnp.float32).astype(jnp.bfloat16) for p in range(slots)], axis=1
        )

    got = jnp.concatenate(
        [
            jnp.concatenate([arrived[pl.ds(f * slots + p, owners, stride=step), :] for f in range(rows)], axis=1)
            for p in range(slots)
        ],
        axis=0,
    )
    old = onehot(old_table)
    grad = sum(dot(old, part, ((1,), (0,))) for part in reversed(thirds(got)))
    updated = []
    for f in range(rows):
        g = grad[:, f * LANES : (f + 1) * LANES]
        first = beta_one * moment_one[f] + (1.0 - beta_one) * g
        second = beta_two * moment_two[f] + (1.0 - beta_two) * g * g
        new_one[f] = first
        new_two[f] = second
        first_hat = first / (1.0 - beta_one**STEP)
        second_hat = second / (1.0 - beta_two**STEP)
        m = master[f]
        m = m - learn_rate * (first_hat / (jnp.sqrt(second_hat) + epsilon) + decay_rate * m)
        new_master[f] = m
        updated.append(m)
    new = onehot(new_table)
    parts = thirds(jnp.concatenate(updated, axis=1))
    picked = sum(dot(new, part, ((0,), (0,))) for part in reversed(parts))
    for f in range(rows):
        for p in range(slots):
            send[pl.ds(f * slots + p, owners, stride=step), :] = picked[
                p * owners : (p + 1) * owners, f * LANES : (f + 1) * LANES
            ]


def product_kernel(place, counts, acts, grads, *refs):
    weights, outputs, input_grads = refs[:-2], refs[-2], refs[-1]
    n = len(weights)
    slots, rows, ff = acts.shape
    for s in range(slots):
        live = lax.broadcasted_iota(jnp.int32, (rows, 1), 0) < counts[s]
        a = halves(jnp.where(live, acts[s], 0.0))
        total = jnp.zeros((rows, ff), jnp.float32)
        for k in range(n):
            block = lax.rem(place[0] + n - k, n)
            columns = pl.ds(pl.multiple_of(block * LANES, LANES), LANES)
            w = halves(weights[k][s])
            outputs[s, :, columns] = dot_split(a, w, ((1,), (0,)))
            g = halves(jnp.where(live, grads[s, :, columns], 0.0))
            total += dot_split(g, w, ((1,), (1,)))
        input_grads[s] = total


VMEM = pl.BlockSpec(memory_space=pltpu.VMEM)
SMEM = pl.BlockSpec(memory_space=pltpu.SMEM)
LIMIT = 40 * 1024 * 1024


def local(
    activations,
    out_grads,
    counts,
    slot_weights,
    master,
    moment_one,
    moment_two,
    old_table,
    new_table,
):
    f32 = jnp.float32
    n = lax.axis_size("dp")
    owners = lax.axis_size("ep")
    me = lax.axis_index("dp")
    slots, tokens, ff = activations.shape
    experts, rows, lanes = master.shape

    def shifted(x, k):
        return lax.ppermute(x, "dp", [(i, (i + k) % n) for i in range(n)])

    shifts = [2, 1, 3]
    acts = {k: shifted(activations, k) for k in shifts}
    positions = jnp.arange(tokens, dtype=jnp.int32)
    live = (positions[None, :] < counts).astype(f32)

    def columns(k):
        block = lax.dynamic_slice_in_dim(out_grads, lax.rem(me + k, n) * lanes, lanes, axis=2)
        return block * live[:, :, None]

    grads = {k: shifted(columns(k), k) for k in shifts}
    column_grad = pl.pallas_call(
        grad_kernel,
        out_shape=jax.ShapeDtypeStruct((slots * ff, lanes), f32),
        in_specs=[VMEM] * (2 * n),
        out_specs=VMEM,
        compiler_params=pltpu.CompilerParams(vmem_limit_bytes=LIMIT),
        name="slot_grads",
    )(activations, *[acts[k] for k in shifts], columns(0), *[grads[k] for k in shifts])
    held, column_grad = lax.optimization_barrier((slot_weights, column_grad))
    near = {k: shifted(held, k) for k in shifts[1:]}
    arrived = lax.all_to_all(
        column_grad.reshape(owners, 1, slots * rows * lanes), "ep", split_axis=0, concat_axis=0, tiled=True
    )
    arrived, near, held = lax.optimization_barrier((arrived, near, held))
    weights = {shifts[0]: shifted(held, shifts[0]), **near}

    plane = jax.ShapeDtypeStruct((rows, experts, lanes), f32)
    flip = lambda x: jnp.transpose(x, (1, 0, 2))
    new_master, new_one, new_two, send = pl.pallas_call(
        adamw_kernel,
        out_shape=(plane, plane, plane, jax.ShapeDtypeStruct((slots * rows * owners, lanes), f32)),
        in_specs=[VMEM] * 6,
        out_specs=(VMEM,) * 4,
        compiler_params=pltpu.CompilerParams(vmem_limit_bytes=LIMIT),
        name="adamw",
    )(
        arrived.reshape(slots * rows * owners, lanes),
        old_table.reshape(owners, slots).T,
        new_table.reshape(owners, slots).T,
        flip(master),
        flip(moment_one),
        flip(moment_two),
    )
    placed = lax.all_to_all(
        send.reshape(owners, 1, slots * rows * lanes), "ep", split_axis=0, concat_axis=0, tiled=True
    )
    outputs, input_grads = pl.pallas_call(
        product_kernel,
        out_shape=(
            jax.ShapeDtypeStruct(out_grads.shape, f32),
            jax.ShapeDtypeStruct(activations.shape, f32),
        ),
        in_specs=[SMEM, SMEM] + [VMEM] * (2 + n),
        out_specs=(VMEM, VMEM),
        compiler_params=pltpu.CompilerParams(vmem_limit_bytes=LIMIT),
        cost_estimate=pl.CostEstimate(flops=12 * slots * tokens * ff * n * lanes, bytes_accessed=8 << 20, transcendentals=0),
        name="products",
    )(
        me.astype(jnp.int32).reshape(1),
        counts[:, 0],
        activations,
        out_grads,
        slot_weights,
        *[weights[k] for k in range(1, n)],
    )
    new_slots = jnp.transpose(placed.reshape(ff, slots, lanes), (1, 0, 2))
    return (outputs, input_grads, flip(new_master), flip(new_one), flip(new_two), new_slots)


def solution(mesh):
    in_specs = (
        P("ep", "dp", None),
        P("ep", "dp", None),
        P("ep", "dp"),
        P("ep", None, "dp"),
        P(None, "ep", "dp"),
        P(None, "ep", "dp"),
        P(None, "ep", "dp"),
        P(),
        P(),
    )
    out_specs = (
        P("ep", "dp", None),
        P("ep", "dp", None),
        P(None, "ep", "dp"),
        P(None, "ep", "dp"),
        P(None, "ep", "dp"),
        P("ep", None, "dp"),
    )
    return jax.shard_map(local, mesh=mesh, in_specs=in_specs, out_specs=out_specs, check_vma=False)
```

```python
import jax
import jax.numpy as jnp
from jax import lax
from jax.experimental import pallas as pl
from jax.experimental.pallas import tpu as pltpu
from jax.sharding import PartitionSpec as P

STEP = 100


beta_one = 0.9
beta_two = 0.999
learn_rate = 0.02
epsilon = 1e-08
decay_rate = 0.1

LANES = 128


def halves(x):
    high = x.astype(jnp.bfloat16)
    low = (x - high.astype(jnp.float32)).astype(jnp.bfloat16)
    return high, low


def thirds(x):
    high = x.astype(jnp.bfloat16)
    rest = x - high.astype(jnp.float32)
    middle = rest.astype(jnp.bfloat16)
    low = (rest - middle.astype(jnp.float32)).astype(jnp.bfloat16)
    return high, middle, low


def dot(a, b, dims):
    return lax.dot_general(a, b, (dims, ((), ())), preferred_element_type=jnp.float32)


def dot_split(a, b, dims):
    (ah, al), (bh, bl) = a, b
    return dot(ah, bh, dims) + (dot(ah, bl, dims) + dot(al, bh, dims))


def pack_kernel(place, counts, acts, grads, *outs):
    n = len(outs)
    slots, rows, ff = acts.shape
    for s in range(slots):
        live = lax.broadcasted_iota(jnp.int32, (rows, 1), 0) < counts[s]
        for k in range(n):
            block = lax.rem(place[0] + k, n)
            columns = pl.ds(pl.multiple_of(block * LANES, LANES), LANES)
            g = jnp.where(live, grads[s, :, columns], 0.0)
            if k:
                outs[k][s, :, :ff] = acts[s]
                outs[k][s, :, ff:] = g
            else:
                outs[k][s] = g


def stacked(acts, grads, others, s):
    ff = acts.shape[2]
    a = jnp.concatenate([acts[s]] + [r[s, :, :ff] for r in others], axis=0)
    g = jnp.concatenate([grads[s]] + [r[s, :, ff:] for r in others], axis=0)
    return halves(a), halves(g)


def grad_kernel(acts, grads, *refs):
    others, out = refs[:-1], refs[-1]
    slots, _, ff = acts.shape
    for s in range(slots):
        a, g = stacked(acts, grads, others, s)
        out[pl.ds(s, ff, stride=slots), :] = dot_split(a, g, ((0,), (0,)))


def product_kernel(after, weights, acts, grads, *refs):
    n = len(refs) // 2 + 1
    others, outs = refs[: n - 1], refs[n - 1 :]
    slots, rows, ff = acts.shape
    for s in range(slots):
        a, g = stacked(acts, grads, others, s)
        w = halves(weights[s])
        columns = dot_split(a, w, ((1,), (0,)))
        part = dot_split(g, w, ((1,), (1,)))
        for k in range(n):
            outs[k][s, :, :ff] = part[k * rows : (k + 1) * rows]
            outs[k][s, :, ff:] = columns[k * rows : (k + 1) * rows]


def combine_kernel(place, counts, *refs):
    n = len(refs) - 2
    parts, outputs, input_grads = refs[:n], refs[-2], refs[-1]
    slots, rows, ff = input_grads.shape
    for s in range(slots):
        live = lax.broadcasted_iota(jnp.int32, (rows, 1), 0) < counts[s]
        total = parts[0][s, :, :ff]
        for k in range(1, n):
            total += parts[k][s, :, :ff]
        input_grads[s] = total
        for k in range(n):
            block = lax.rem(place[0] + k, n)
            columns = pl.ds(pl.multiple_of(block * LANES, LANES), LANES)
            outputs[s, :, columns] = jnp.where(live, parts[k][s, :, ff:], 0.0)


def place_kernel(rows, out):
    slots, ff, _ = out.shape
    for s in range(slots):
        out[s] = rows[pl.ds(s, ff, stride=slots), :]


def adamw_kernel(after, arrived, old_table, new_table, master_in, one_in, two_in,
                 new_master, new_one, new_two, send, master, moment_one, moment_two, arrivals):
    copies = [
        pltpu.make_async_copy(there, here, arrivals.at[i])
        for i, (there, here) in enumerate([(master_in, master), (one_in, moment_one), (two_in, moment_two)])
    ]
    for copy in copies:
        copy.start()
    rows, experts, _ = master.shape
    slots, owners = old_table.shape
    step = rows * slots
    ids = lax.broadcasted_iota(jnp.int32, (experts, owners), 0)

    def onehot(table):
        return jnp.concatenate(
            [(ids == table[p : p + 1, :]).astype(jnp.float32).astype(jnp.bfloat16) for p in range(slots)], axis=1
        )

    got = jnp.concatenate(
        [
            jnp.concatenate([arrived[pl.ds(f * slots + p, owners, stride=step), :] for f in range(rows)], axis=1)
            for p in range(slots)
        ],
        axis=0,
    )
    old = onehot(old_table)
    grad = sum(dot(old, part, ((1,), (0,))) for part in reversed(thirds(got)))
    for copy in copies:
        copy.wait()
    updated = []
    for f in range(rows):
        g = grad[:, f * LANES : (f + 1) * LANES]
        first = beta_one * moment_one[f] + (1.0 - beta_one) * g
        second = beta_two * moment_two[f] + (1.0 - beta_two) * g * g
        new_one[f] = first
        new_two[f] = second
        first_hat = first / (1.0 - beta_one**STEP)
        second_hat = second / (1.0 - beta_two**STEP)
        m = master[f]
        m = m - learn_rate * (first_hat / (jnp.sqrt(second_hat) + epsilon) + decay_rate * m)
        new_master[f] = m
        updated.append(m)
    new = onehot(new_table)
    parts = thirds(jnp.concatenate(updated, axis=1))
    picked = sum(dot(new, part, ((0,), (0,))) for part in reversed(parts))
    for f in range(rows):
        for p in range(slots):
            send[pl.ds(f * slots + p, owners, stride=step), :] = picked[
                p * owners : (p + 1) * owners, f * LANES : (f + 1) * LANES
            ]


VMEM = pl.BlockSpec(memory_space=pltpu.VMEM)
SMEM = pl.BlockSpec(memory_space=pltpu.SMEM)
ANY = pl.BlockSpec(memory_space=pl.ANY)
SOME = 24 * 1024 * 1024
MOST = 60 * 1024 * 1024


def kernel(body, out_shape, in_specs, name, scratch=(), flops=0, limit=SOME):
    alone = not isinstance(out_shape, tuple)
    return pl.pallas_call(
        body,
        out_shape=out_shape,
        in_specs=in_specs,
        out_specs=VMEM if alone else (VMEM,) * len(out_shape),
        scratch_shapes=scratch,
        compiler_params=pltpu.CompilerParams(vmem_limit_bytes=limit),
        cost_estimate=pl.CostEstimate(flops=flops, bytes_accessed=4 << 20, transcendentals=0),
        name=name,
    )


def local(
    activations,
    out_grads,
    counts,
    slot_weights,
    master,
    moment_one,
    moment_two,
    old_table,
    new_table,
):
    f32 = jnp.float32
    n = lax.axis_size("dp")
    owners = lax.axis_size("ep")
    me = lax.axis_index("dp")
    slots, tokens, ff = activations.shape
    experts, rows, lanes = master.shape

    def shifted(x, k):
        return lax.ppermute(x, "dp", [(i, (i + k) % n) for i in range(n)])

    def shape(*dims):
        return jax.ShapeDtypeStruct(dims, f32)

    place = me.astype(jnp.int32).reshape(1)
    limits = counts[:, 0]
    far = n // 2
    shifts = [far] + [k for k in range(1, n) if k != far]
    packet = shape(slots, tokens, ff + lanes)
    work = 6 * slots * tokens * n * ff * lanes

    own, *packed = kernel(
        pack_kernel, (shape(slots, tokens, lanes),) + (packet,) * (n - 1), [SMEM, SMEM, VMEM, VMEM], "pack", limit=MOST
    )(place, limits, activations, out_grads)
    came = {k: shifted(packed[k - 1], k) for k in shifts}
    others = [came[k] for k in range(1, n)]
    column_grad = kernel(grad_kernel, shape(slots * ff, lanes), [VMEM] * (n + 1), "slot_grads", flops=work)(
        activations, own, *others
    )
    arrived = lax.all_to_all(
        column_grad.reshape(owners, 1, slots * rows * lanes), "ep", split_axis=0, concat_axis=0, tiled=True
    )
    kept, *parts = kernel(product_kernel, (packet,) * n, [ANY] + [VMEM] * (n + 2), "products", flops=2 * work)(
        column_grad, slot_weights, activations, own, *others
    )
    back = {k: shifted(parts[k - 1], n - k) for k in shifts}

    plane = shape(rows, experts, lanes)
    flip = lambda x: jnp.transpose(x, (1, 0, 2))
    new_master, new_one, new_two, send = kernel(
        adamw_kernel,
        (plane, plane, plane, shape(slots * rows * owners, lanes)),
        [ANY] + [VMEM] * 3 + [ANY] * 3,
        "adamw",
        scratch=[pltpu.VMEM(plane.shape, f32)] * 3 + [pltpu.SemaphoreType.DMA((3,))],
        flops=work,
        limit=MOST,
    )(
        back[far],
        arrived.reshape(slots * rows * owners, lanes),
        old_table.reshape(owners, slots).T,
        new_table.reshape(owners, slots).T,
        flip(master),
        flip(moment_one),
        flip(moment_two),
    )
    placed = lax.all_to_all(
        send.reshape(owners, 1, slots * rows * lanes), "ep", split_axis=0, concat_axis=0, tiled=True
    )
    outputs, input_grads = kernel(
        combine_kernel, (shape(*out_grads.shape), shape(*activations.shape)), [SMEM, SMEM] + [VMEM] * n, "combine"
    )(place, limits, kept, *[back[k] for k in range(1, n)])
    new_slots = kernel(place_kernel, shape(*slot_weights.shape), [VMEM], "new_slots")(
        placed.reshape(ff * slots, lanes)
    )
    return (outputs, input_grads, flip(new_master), flip(new_one), flip(new_two), new_slots)


def solution(mesh):
    in_specs = (
        P("ep", "dp", None),
        P("ep", "dp", None),
        P("ep", "dp"),
        P("ep", None, "dp"),
        P(None, "ep", "dp"),
        P(None, "ep", "dp"),
        P(None, "ep", "dp"),
        P(),
        P(),
    )
    out_specs = (
        P("ep", "dp", None),
        P("ep", "dp", None),
        P(None, "ep", "dp"),
        P(None, "ep", "dp"),
        P(None, "ep", "dp"),
        P("ep", None, "dp"),
    )
    return jax.shard_map(local, mesh=mesh, in_specs=in_specs, out_specs=out_specs, check_vma=False)
```

```python
import jax
import jax.numpy as jnp
from jax import lax
from jax.experimental import pallas as pl
from jax.experimental.pallas import tpu as pltpu
from jax.sharding import PartitionSpec as P

STEP = 100


beta_one = 0.9
beta_two = 0.999
learn_rate = 0.02
epsilon = 1e-08
decay_rate = 0.1

LANES = 128


def halves(x):
    high = x.astype(jnp.bfloat16)
    low = (x - high.astype(jnp.float32)).astype(jnp.bfloat16)
    return high, low


def thirds(x):
    high = x.astype(jnp.bfloat16)
    rest = x - high.astype(jnp.float32)
    middle = rest.astype(jnp.bfloat16)
    low = (rest - middle.astype(jnp.float32)).astype(jnp.bfloat16)
    return high, middle, low


def dot(a, b, dims):
    return lax.dot_general(a, b, (dims, ((), ())), preferred_element_type=jnp.float32)


def dot_split(a, b, dims):
    (ah, al), (bh, bl) = a, b
    return dot(ah, bh, dims) + (dot(ah, bl, dims) + dot(al, bh, dims))


CUT = LANES


def own_columns(place, counts, grads, s, k=0):
    n = grads.shape[2] // LANES
    live = lax.broadcasted_iota(jnp.int32, (grads.shape[1], 1), 0) < counts[s]
    block = lax.rem(place[0] + k, n)
    columns = pl.ds(pl.multiple_of(block * LANES, LANES), LANES)
    return jnp.where(live, grads[s, :, columns], 0.0)


def pack_kernel(place, counts, acts, grads, ahead, behind, opposite):
    slots, _, ff = acts.shape
    for s in range(slots):
        ahead[s, :, :ff] = acts[s]
        ahead[s, :, ff:] = own_columns(place, counts, grads, s, 1)
        behind[s, :, :ff] = acts[s]
        behind[s, :, ff:] = own_columns(place, counts, grads, s, 3)
        opposite[s, :, :CUT] = acts[s, :, :CUT]
        opposite[s, :, CUT:] = own_columns(place, counts, grads, s, 2)


def stacked(place, counts, acts, grads, ahead, behind, opposite, relayed, s):
    ff = acts.shape[2]
    far = jnp.concatenate([opposite[s, :, :CUT], relayed[s]], axis=1)
    a = jnp.concatenate([acts[s], ahead[s, :, :ff], far, behind[s, :, :ff]], axis=0)
    g = jnp.concatenate(
        [own_columns(place, counts, grads, s), ahead[s, :, ff:], opposite[s, :, CUT:], behind[s, :, ff:]], axis=0
    )
    return halves(a), halves(g)


def grad_kernel(*refs):
    given, out = refs[:-1], refs[-1]
    slots, _, ff = given[2].shape
    for s in range(slots):
        a, g = stacked(*given, s)
        out[pl.ds(s, ff, stride=slots), :] = dot_split(a, g, ((0,), (0,)))


def product_kernel(after, weights, *refs):
    given, outs = refs[:8], refs[8:]
    slots, rows, ff = given[2].shape
    for s in range(slots):
        a, g = stacked(*given, s)
        w = halves(weights[s])
        columns = dot_split(a, w, ((1,), (0,)))
        part = dot_split(g, w, ((1,), (1,)))
        for k, out in enumerate(outs):
            out[s, :, :ff] = part[k * rows : (k + 1) * rows]
            out[s, :, ff:] = columns[k * rows : (k + 1) * rows]


def combine_kernel(place, counts, *refs):
    n = len(refs) - 2
    parts, outputs, input_grads = refs[:n], refs[-2], refs[-1]
    slots, rows, ff = input_grads.shape
    for s in range(slots):
        live = lax.broadcasted_iota(jnp.int32, (rows, 1), 0) < counts[s]
        total = parts[0][s, :, :ff]
        for k in range(1, n):
            total += parts[k][s, :, :ff]
        input_grads[s] = total
        for k in range(n):
            block = lax.rem(place[0] + k, n)
            columns = pl.ds(pl.multiple_of(block * LANES, LANES), LANES)
            outputs[s, :, columns] = jnp.where(live, parts[k][s, :, ff:], 0.0)


def place_kernel(rows, out):
    slots, ff, _ = out.shape
    for s in range(slots):
        out[s] = rows[pl.ds(s, ff, stride=slots), :]


PIECES = 4


def adamw_kernel(after, arrived_in, old_table, new_table, master_in, one_in, two_in,
                 master_out, one_out, two_out, send_out,
                 arrived, master, moment_one, moment_two, new_master, new_one, new_two, send, landed, left):
    def moves(pairs, signals, first=0):
        return [pltpu.make_async_copy(a, b, signals.at[first + i]) for i, (a, b) in enumerate(pairs)]

    def split(a, b):
        part = a.shape[0] // PIECES
        return [(a.at[pl.ds(i * part, part)], b.at[pl.ds(i * part, part)]) for i in range(PIECES)]

    early = moves(split(arrived_in, arrived), landed)
    later = moves([(master_in, master), (one_in, moment_one), (two_in, moment_two)], landed, PIECES)
    for copy in early + later:
        copy.start()
    rows, experts, _ = master.shape
    slots, owners = old_table.shape
    step = rows * slots
    ids = lax.broadcasted_iota(jnp.int32, (experts, owners), 0)

    def onehot(table):
        return jnp.concatenate(
            [(ids == table[p : p + 1, :]).astype(jnp.float32).astype(jnp.bfloat16) for p in range(slots)], axis=1
        )

    old = onehot(old_table)
    new = onehot(new_table)
    for copy in early:
        copy.wait()
    got = jnp.concatenate(
        [
            jnp.concatenate([arrived[pl.ds(f * slots + p, owners, stride=step), :] for f in range(rows)], axis=1)
            for p in range(slots)
        ],
        axis=0,
    )
    grad = sum(dot(old, part, ((1,), (0,))) for part in reversed(thirds(got)))
    for copy in later:
        copy.wait()
    updated = []
    for f in range(rows):
        g = grad[:, f * LANES : (f + 1) * LANES]
        first = beta_one * moment_one[f] + (1.0 - beta_one) * g
        second = beta_two * moment_two[f] + (1.0 - beta_two) * g * g
        new_one[f] = first
        new_two[f] = second
        first_hat = first / (1.0 - beta_one**STEP)
        second_hat = second / (1.0 - beta_two**STEP)
        m = master[f]
        m = m - learn_rate * (first_hat / (jnp.sqrt(second_hat) + epsilon) + decay_rate * m)
        new_master[f] = m
        updated.append(m)
    results = moves([(new_master, master_out), (new_one, one_out), (new_two, two_out)], left, PIECES)
    for copy in results:
        copy.start()
    parts = thirds(jnp.concatenate(updated, axis=1))
    picked = sum(dot(new, part, ((0,), (0,))) for part in reversed(parts))
    for f in range(rows):
        for p in range(slots):
            send[pl.ds(f * slots + p, owners, stride=step), :] = picked[
                p * owners : (p + 1) * owners, f * LANES : (f + 1) * LANES
            ]
    sent = moves(split(send, send_out), left)
    for copy in sent:
        copy.start()
    for copy in results + sent:
        copy.wait()


VMEM = pl.BlockSpec(memory_space=pltpu.VMEM)
SMEM = pl.BlockSpec(memory_space=pltpu.SMEM)
ANY = pl.BlockSpec(memory_space=pl.ANY)
SOME = 24 * 1024 * 1024
MOST = 60 * 1024 * 1024


def kernel(body, out_shape, in_specs, name, flops=0, limit=SOME, spec=VMEM, scratch=()):
    alone = not isinstance(out_shape, tuple)
    return pl.pallas_call(
        body,
        out_shape=out_shape,
        in_specs=in_specs,
        out_specs=spec if alone else (spec,) * len(out_shape),
        scratch_shapes=scratch,
        compiler_params=pltpu.CompilerParams(vmem_limit_bytes=limit),
        cost_estimate=pl.CostEstimate(flops=flops, bytes_accessed=4 << 20, transcendentals=0),
        name=name,
    )


def local(
    activations,
    out_grads,
    counts,
    slot_weights,
    master,
    moment_one,
    moment_two,
    old_table,
    new_table,
):
    f32 = jnp.float32
    n = lax.axis_size("dp")
    owners = lax.axis_size("ep")
    me = lax.axis_index("dp")
    slots, tokens, ff = activations.shape
    experts, rows, lanes = master.shape

    def shifted(x, k):
        return lax.ppermute(x, "dp", [(i, (i + k) % n) for i in range(n)])

    def shape(*dims):
        return jax.ShapeDtypeStruct(dims, f32)

    place = me.astype(jnp.int32).reshape(1)
    limits = counts[:, 0]
    far = n // 2
    shifts = [far] + [k for k in range(1, n) if k != far]
    packet = shape(slots, tokens, ff + lanes)
    work = 6 * slots * tokens * n * ff * lanes

    ahead, behind, opposite = kernel(
        pack_kernel,
        (packet, packet, shape(slots, tokens, CUT + lanes)),
        [SMEM, SMEM, VMEM, VMEM],
        "pack",
        limit=MOST,
    )(place, limits, activations, out_grads)
    ahead = shifted(ahead, 1)
    behind = shifted(behind, n - 1)
    opposite = shifted(opposite, far)
    relayed = shifted(ahead[:, :, CUT:ff], 1)
    given = (place, limits, activations, out_grads, ahead, behind, opposite, relayed)
    column_grad = kernel(grad_kernel, shape(slots * ff, lanes), [SMEM] * 2 + [VMEM] * 6, "slot_grads", flops=work)(
        *given
    )
    arrived = lax.all_to_all(
        column_grad.reshape(owners, 1, slots * rows * lanes), "ep", split_axis=0, concat_axis=0, tiled=True
    )
    kept, *parts = kernel(
        product_kernel, (packet,) * n, [ANY, VMEM, SMEM, SMEM] + [VMEM] * 6, "products", flops=2 * work
    )(column_grad, slot_weights, *given)
    back = {k: shifted(parts[k - 1], n - k) for k in shifts}

    plane = shape(rows, experts, lanes)
    flip = lambda x: jnp.transpose(x, (1, 0, 2))
    new_master, new_one, new_two, send = kernel(
        adamw_kernel,
        (plane, plane, plane, shape(slots * rows * owners, lanes)),
        [ANY, ANY, VMEM, VMEM, ANY, ANY, ANY],
        "adamw",
        flops=work,
        limit=MOST,
        spec=ANY,
        scratch=[pltpu.VMEM((slots * rows * owners, lanes), f32)]
        + [pltpu.VMEM(plane.shape, f32)] * 6
        + [pltpu.VMEM((slots * rows * owners, lanes), f32)]
        + [pltpu.SemaphoreType.DMA((PIECES + 3,))] * 2,
    )(
        back[far],
        arrived.reshape(slots * rows * owners, lanes),
        old_table.reshape(owners, slots).T,
        new_table.reshape(owners, slots).T,
        flip(master),
        flip(moment_one),
        flip(moment_two),
    )
    placed = lax.all_to_all(
        send.reshape(owners, 1, slots * rows * lanes), "ep", split_axis=0, concat_axis=0, tiled=True
    )
    outputs, input_grads = kernel(
        combine_kernel, (shape(*out_grads.shape), shape(*activations.shape)), [SMEM, SMEM] + [VMEM] * n, "combine"
    )(place, limits, kept, *[back[k] for k in range(1, n)])
    new_slots = kernel(place_kernel, shape(*slot_weights.shape), [VMEM], "new_slots")(
        placed.reshape(ff * slots, lanes)
    )
    return (outputs, input_grads, flip(new_master), flip(new_one), flip(new_two), new_slots)


def solution(mesh):
    in_specs = (
        P("ep", "dp", None),
        P("ep", "dp", None),
        P("ep", "dp"),
        P("ep", None, "dp"),
        P(None, "ep", "dp"),
        P(None, "ep", "dp"),
        P(None, "ep", "dp"),
        P(),
        P(),
    )
    out_specs = (
        P("ep", "dp", None),
        P("ep", "dp", None),
        P(None, "ep", "dp"),
        P(None, "ep", "dp"),
        P(None, "ep", "dp"),
        P("ep", None, "dp"),
    )
    return jax.shard_map(local, mesh=mesh, in_specs=in_specs, out_specs=out_specs, check_vma=False)
```

```python
import jax
import jax.numpy as jnp
from jax import lax
from jax.experimental import pallas as pl
from jax.experimental.pallas import tpu as pltpu
from jax.sharding import Mesh, PartitionSpec as P

STEP = 100


beta_one = 0.9
beta_two = 0.999
learn_rate = 0.02
epsilon = 1e-08
decay_rate = 0.1

LANES = 128
PIECES = 4


def halves(x):
    high = x.astype(jnp.bfloat16)
    low = (x - high.astype(jnp.float32)).astype(jnp.bfloat16)
    return high, low


def thirds(x):
    high = x.astype(jnp.bfloat16)
    rest = x - high.astype(jnp.float32)
    middle = rest.astype(jnp.bfloat16)
    low = (rest - middle.astype(jnp.float32)).astype(jnp.bfloat16)
    return high, middle, low


def dot(a, b, dims):
    return lax.dot_general(a, b, (dims, ((), ())), preferred_element_type=jnp.float32)


def dot_split(a, b, dims):
    (ah, al), (bh, bl) = a, b
    return dot(ah, bh, dims) + (dot(ah, bl, dims) + dot(al, bh, dims))


def pack_kernel(counts, acts, grads, out):
    slots, rows, ff = acts.shape
    half = grads.shape[2] // slots
    for s in range(slots):
        live = lax.broadcasted_iota(jnp.int32, (rows, 1), 0) < counts[s]
        for b in range(slots):
            out[slots * b + s, :, :ff] = acts[s]
            out[slots * b + s, :, ff:] = jnp.where(live, grads[s, :, b * half : (b + 1) * half], 0.0)


def rows_of(came, ff):
    n, rows, width = came.shape
    a = came[:, :, :ff].reshape(n * rows, ff)
    g = came[:, :, ff:].reshape(n * rows, width - ff)
    return halves(a), halves(g)


def grad_kernel(came, out):
    ff = out.shape[0] // 2
    a, g = rows_of(came, ff)
    grad = dot_split(a, g, ((0,), (0,)))
    out[:ff] = grad[:, :LANES]
    out[ff:] = grad[:, LANES:]


def swap_kernel(after, slot, weights, out):
    out[...] = weights[1 - slot[0]]


def product_kernel(place, weights, other, came, *refs):
    outs, whole = refs[:-1], refs[-1]
    n, rows, _ = came.shape
    ff = weights.shape[1]
    slot = lax.rem(place[0], 2)
    mine, theirs = weights[slot], other[...]
    first = slot == 0
    w = halves(jnp.concatenate([jnp.where(first, mine, theirs), jnp.where(first, theirs, mine)], axis=1))
    a, g = rows_of(came, ff)
    whole[:, ff:] = dot_split(a, w, ((1,), (0,)))
    whole[:, :ff] = dot_split(g, w, ((1,), (1,)))
    for k, out in enumerate(outs):
        owner = lax.rem(place[0] + k, n)
        out[...] = whole[pl.ds(pl.multiple_of(owner * rows, rows), rows), :]


def combine_kernel(place, counts, *refs):
    parts, outputs, input_grads, whole = refs[:-3], refs[-3], refs[-2], refs[-1]
    n = len(parts)
    slots, rows, ff = input_grads.shape
    half = outputs.shape[2] // slots
    for k in range(n):
        whole[lax.rem(place[0] + n - k, n)] = parts[k][...]
    for s in range(slots):
        live = lax.broadcasted_iota(jnp.int32, (rows, 1), 0) < counts[s]
        input_grads[s] = whole[s, :, :ff] + whole[slots + s, :, :ff]
        for b in range(slots):
            outputs[s, :, b * half : (b + 1) * half] = jnp.where(live, whole[slots * b + s, :, ff:], 0.0)


def place_kernel(rows, out):
    slots, ff, _ = out.shape
    for s in range(slots):
        out[s] = rows[pl.ds(s, ff, stride=slots), :]


def adamw_kernel(after, arrived_in, old_table, new_table, master_in, one_in, two_in,
                 master_out, one_out, two_out, send_out,
                 arrived, master, moment_one, moment_two, new_master, new_one, new_two, send, landed, left):
    def moves(pairs, signals, first=0):
        return [pltpu.make_async_copy(a, b, signals.at[first + i]) for i, (a, b) in enumerate(pairs)]

    def split(a, b):
        part = a.shape[0] // PIECES
        return [(a.at[pl.ds(i * part, part)], b.at[pl.ds(i * part, part)]) for i in range(PIECES)]

    early = moves(split(arrived_in, arrived), landed)
    later = moves([(master_in, master), (one_in, moment_one), (two_in, moment_two)], landed, PIECES)
    for copy in early + later:
        copy.start()
    rows, experts, _ = master.shape
    total = old_table.shape[1]
    slots = 2
    owners = total // slots
    source = lax.broadcasted_iota(jnp.int32, (total, total), 0)
    target = lax.broadcasted_iota(jnp.int32, (total, total), 1)
    wanted = slots * lax.rem(target, owners) + target // owners
    order = (source == wanted).astype(jnp.float32).astype(jnp.bfloat16)
    ids = lax.broadcasted_iota(jnp.int32, (experts, total), 0)

    def onehot(table):
        named = jnp.broadcast_to(table[...].astype(jnp.float32), (8, total)).astype(jnp.bfloat16)
        named = dot(named, order, ((1,), (0,)))[:1].astype(jnp.int32)
        return (ids == named).astype(jnp.float32).astype(jnp.bfloat16)

    old = onehot(old_table)
    new = onehot(new_table)
    for copy in early:
        copy.wait()
    got = jnp.concatenate([arrived[pl.ds(f, total, stride=rows), :] for f in range(rows)], axis=1)
    grad = sum(dot(old, part, ((1,), (0,))) for part in reversed(thirds(got)))
    for copy in later:
        copy.wait()
    updated = []
    for f in range(rows):
        g = grad[:, f * LANES : (f + 1) * LANES]
        first = beta_one * moment_one[f] + (1.0 - beta_one) * g
        second = beta_two * moment_two[f] + (1.0 - beta_two) * g * g
        new_one[f] = first
        new_two[f] = second
        first_hat = first / (1.0 - beta_one**STEP)
        second_hat = second / (1.0 - beta_two**STEP)
        m = master[f]
        m = m - learn_rate * (first_hat / (jnp.sqrt(second_hat) + epsilon) + decay_rate * m)
        new_master[f] = m
        updated.append(m)
    results = moves([(new_master, master_out), (new_one, one_out), (new_two, two_out)], left, PIECES)
    for copy in results:
        copy.start()
    parts = thirds(jnp.concatenate(updated, axis=1))
    picked = sum(dot(new, part, ((0,), (0,))) for part in reversed(parts))
    for f in range(rows):
        for p in range(slots):
            send[pl.ds(f * slots + p, owners, stride=rows * slots), :] = picked[
                p * owners : (p + 1) * owners, f * LANES : (f + 1) * LANES
            ]
    sent = moves(split(send, send_out), left)
    for copy in sent:
        copy.start()
    for copy in results + sent:
        copy.wait()


VMEM = pl.BlockSpec(memory_space=pltpu.VMEM)
SMEM = pl.BlockSpec(memory_space=pltpu.SMEM)
ANY = pl.BlockSpec(memory_space=pl.ANY)
SOME = 24 * 1024 * 1024
MOST = 60 * 1024 * 1024


def kernel(body, out_shape, in_specs, name, flops=0, limit=SOME, spec=VMEM, scratch=()):
    alone = not isinstance(out_shape, tuple)
    return pl.pallas_call(
        body,
        out_shape=out_shape,
        in_specs=in_specs,
        out_specs=spec if alone else (spec,) * len(out_shape),
        scratch_shapes=scratch,
        compiler_params=pltpu.CompilerParams(vmem_limit_bytes=limit),
        cost_estimate=pl.CostEstimate(flops=flops, bytes_accessed=4 << 20, transcendentals=0),
        name=name,
    )


def local(
    activations,
    out_grads,
    counts,
    slot_weights,
    master,
    moment_one,
    moment_two,
    old_table,
    new_table,
):
    f32 = jnp.float32
    dp = ("half", "slot")
    n = lax.axis_size("half") * lax.axis_size("slot")
    owners = lax.axis_size("ep")
    me = lax.axis_index("half") * lax.axis_size("slot") + lax.axis_index("slot")
    slots, tokens, ff = activations.shape
    experts, rows, lanes = master.shape
    width = ff + slots * lanes

    def shape(*dims):
        return jax.ShapeDtypeStruct(dims, f32)

    def scalar(x):
        return x.astype(jnp.int32).reshape(1)

    def exchange(x, axes):
        return lax.all_to_all(x, axes, split_axis=0, concat_axis=0, tiled=True)

    place = scalar(me)
    limits = counts[:, 0]
    packet = shape(tokens, width)
    work = 6 * slots * tokens * n * ff * lanes

    packed = kernel(pack_kernel, shape(n, tokens, width), [SMEM, VMEM, VMEM], "pack", limit=MOST)(
        limits, activations, out_grads
    )
    came = exchange(packed, dp)
    column_grad = kernel(grad_kernel, shape(slots * ff, lanes), [VMEM], "slot_grads", flops=work)(came)
    arrived = exchange(column_grad.reshape(slots * owners, 1, rows * lanes), ("slot", "ep"))

    given = kernel(swap_kernel, shape(ff, lanes), [ANY, SMEM, VMEM], "swap")(
        column_grad, scalar(lax.axis_index("slot")), slot_weights
    )
    other = lax.ppermute(given, "slot", [(0, 1), (1, 0)])
    parts = kernel(
        product_kernel,
        (packet,) * n,
        [SMEM, VMEM, VMEM, VMEM],
        "products",
        flops=2 * work,
        scratch=[pltpu.VMEM((n * tokens, width), f32)],
    )(place, slot_weights, other, came)

    plane = shape(rows, experts, lanes)
    flat = shape(slots * rows * owners, lanes)
    flip = lambda x: jnp.transpose(x, (1, 0, 2))
    new_master, new_one, new_two, send = kernel(
        adamw_kernel,
        (plane, plane, plane, flat),
        [ANY, ANY, VMEM, VMEM, ANY, ANY, ANY],
        "adamw",
        flops=work,
        limit=MOST,
        spec=ANY,
        scratch=[pltpu.VMEM(flat.shape, f32)]
        + [pltpu.VMEM(plane.shape, f32)] * 6
        + [pltpu.VMEM(flat.shape, f32)]
        + [pltpu.SemaphoreType.DMA((PIECES + 3,))] * 2,
    )(
        parts[0],
        arrived.reshape(flat.shape),
        old_table.T,
        new_table.T,
        flip(master),
        flip(moment_one),
        flip(moment_two),
    )
    placed = exchange(send.reshape(owners, 1, slots * rows * lanes), "ep")
    back = [parts[0]] + [
        lax.ppermute(parts[k], dp, [(i, (i + k) % n) for i in range(n)]) for k in range(1, n)
    ]
    outputs, input_grads = kernel(
        combine_kernel,
        (shape(*out_grads.shape), shape(*activations.shape)),
        [SMEM, SMEM] + [VMEM] * n,
        "combine",
        scratch=[pltpu.VMEM((n, tokens, width), f32)],
    )(place, limits, *back)
    new_slots = kernel(place_kernel, shape(*slot_weights.shape), [VMEM], "new_slots")(
        placed.reshape(ff * slots, lanes)
    )
    return (outputs, input_grads, flip(new_master), flip(new_one), flip(new_two), new_slots)


def solution(mesh):
    ep, dp = mesh.devices.shape
    split = Mesh(mesh.devices.reshape(ep, dp // 2, 2), ("ep", "half", "slot"))
    both = ("half", "slot")
    in_specs = (
        P("ep", both, None),
        P("ep", both, None),
        P("ep", both),
        P("ep", None, both),
        P(None, "ep", both),
        P(None, "ep", both),
        P(None, "ep", both),
        P(),
        P(),
    )
    out_specs = (
        P("ep", both, None),
        P("ep", both, None),
        P(None, "ep", both),
        P(None, "ep", both),
        P(None, "ep", both),
        P("ep", None, both),
    )
    return jax.shard_map(local, mesh=split, in_specs=in_specs, out_specs=out_specs, check_vma=False)
```

```python
import jax
import jax.numpy as jnp
from jax import lax
from jax.experimental import pallas as pl
from jax.experimental.pallas import tpu as pltpu
from jax.sharding import Mesh, PartitionSpec as P

STEP = 100


beta_one = 0.9
beta_two = 0.999
learn_rate = 0.02
epsilon = 1e-08
decay_rate = 0.1

LANES = 128
PIECES = 4


def halves(x):
    high = x.astype(jnp.bfloat16)
    low = (x - high.astype(jnp.float32)).astype(jnp.bfloat16)
    return high, low


def thirds(x):
    high = x.astype(jnp.bfloat16)
    rest = x - high.astype(jnp.float32)
    middle = rest.astype(jnp.bfloat16)
    low = (rest - middle.astype(jnp.float32)).astype(jnp.bfloat16)
    return high, middle, low


def dot(a, b, dims):
    return lax.dot_general(a, b, (dims, ((), ())), preferred_element_type=jnp.float32)


def dot_split(a, b, dims):
    (ah, al), (bh, bl) = a, b
    return dot(ah, bh, dims) + (dot(ah, bl, dims) + dot(al, bh, dims))


def pack_kernel(counts, acts, grads, out):
    slots, rows, ff = acts.shape
    half = grads.shape[2] // slots
    for s in range(slots):
        live = lax.broadcasted_iota(jnp.int32, (rows, 1), 0) < counts[s]
        for b in range(slots):
            out[slots * b + s, :, :ff] = acts[s]
            out[slots * b + s, :, ff:] = jnp.where(live, grads[s, :, b * half : (b + 1) * half], 0.0)


def rows_of(came, ff):
    n, rows, width = came.shape
    a = came[:, :, :ff].reshape(n * rows, ff)
    g = came[:, :, ff:].reshape(n * rows, width - ff)
    return halves(a), halves(g)


def grad_kernel(came, out):
    ff = out.shape[0] // 2
    a, g = rows_of(came, ff)
    grad = dot_split(a, g, ((0,), (0,)))
    out[:ff] = grad[:, :LANES]
    out[ff:] = grad[:, LANES:]


def swap_kernel(after, slot, weights, out):
    out[...] = weights[1 - slot[0]]


def product_kernel(after, place, weights, other, came, *refs):
    outs, whole = refs[:-1], refs[-1]
    n, rows, _ = came.shape
    ff = weights.shape[1]
    slot = lax.rem(place[0], 2)
    mine, theirs = weights[slot], other[...]
    first = slot == 0
    w = halves(jnp.concatenate([jnp.where(first, mine, theirs), jnp.where(first, theirs, mine)], axis=1))
    a, g = rows_of(came, ff)
    whole[:, ff:] = dot_split(a, w, ((1,), (0,)))
    whole[:, :ff] = dot_split(g, w, ((1,), (1,)))
    for k, out in enumerate(outs):
        owner = lax.rem(place[0] + k, n)
        out[...] = whole[pl.ds(pl.multiple_of(owner * rows, rows), rows), :]


def combine_kernel(place, counts, *refs):
    parts, outputs, input_grads, whole = refs[:-3], refs[-3], refs[-2], refs[-1]
    n = len(parts)
    slots, rows, ff = input_grads.shape
    half = outputs.shape[2] // slots
    for k in range(n):
        whole[lax.rem(place[0] + n - k, n)] = parts[k][...]
    for s in range(slots):
        live = lax.broadcasted_iota(jnp.int32, (rows, 1), 0) < counts[s]
        input_grads[s] = whole[s, :, :ff] + whole[slots + s, :, :ff]
        for b in range(slots):
            outputs[s, :, b * half : (b + 1) * half] = jnp.where(live, whole[slots * b + s, :, ff:], 0.0)


def place_kernel(rows, out):
    slots, ff, _ = out.shape
    for s in range(slots):
        out[s] = rows[pl.ds(s, ff, stride=slots), :]


def adamw_kernel(after, arrived_in, old_in, new_in, master_in, one_in, two_in,
                 master_out, one_out, two_out, send_out,
                 arrived, old_table, new_table, master, moment_one, moment_two, new_master, new_one, new_two, send, landed, left):
    def moves(pairs, signals, first=0):
        return [pltpu.make_async_copy(a, b, signals.at[first + i]) for i, (a, b) in enumerate(pairs)]

    def split(a, b):
        part = a.shape[0] // PIECES
        return [(a.at[pl.ds(i * part, part)], b.at[pl.ds(i * part, part)]) for i in range(PIECES)]

    tables = moves([(old_in, old_table), (new_in, new_table)], landed, PIECES + 3)
    early = moves(split(arrived_in, arrived), landed)
    later = moves([(master_in, master), (one_in, moment_one), (two_in, moment_two)], landed, PIECES)
    for copy in tables + early + later:
        copy.start()
    rows, experts, _ = master.shape
    total = old_table.shape[1]
    slots = 2
    owners = total // slots
    source = lax.broadcasted_iota(jnp.int32, (total, total), 0)
    target = lax.broadcasted_iota(jnp.int32, (total, total), 1)
    wanted = slots * lax.rem(target, owners) + target // owners
    order = (source == wanted).astype(jnp.float32).astype(jnp.bfloat16)
    ids = lax.broadcasted_iota(jnp.int32, (experts, total), 0)

    def onehot(table):
        named = jnp.broadcast_to(table[...].astype(jnp.float32), (8, total)).astype(jnp.bfloat16)
        named = dot(named, order, ((1,), (0,)))[:1].astype(jnp.int32)
        return (ids == named).astype(jnp.float32).astype(jnp.bfloat16)

    for copy in tables:
        copy.wait()
    old = onehot(old_table)
    new = onehot(new_table)
    for copy in early:
        copy.wait()
    got = jnp.concatenate([arrived[pl.ds(f, total, stride=rows), :] for f in range(rows)], axis=1)
    grad = sum(dot(old, part, ((1,), (0,))) for part in reversed(thirds(got)))
    for copy in later:
        copy.wait()
    updated = []
    for f in range(rows):
        g = grad[:, f * LANES : (f + 1) * LANES]
        first = beta_one * moment_one[f] + (1.0 - beta_one) * g
        second = beta_two * moment_two[f] + (1.0 - beta_two) * g * g
        new_one[f] = first
        new_two[f] = second
        first_hat = first / (1.0 - beta_one**STEP)
        second_hat = second / (1.0 - beta_two**STEP)
        m = master[f]
        m = m - learn_rate * (first_hat / (jnp.sqrt(second_hat) + epsilon) + decay_rate * m)
        new_master[f] = m
        updated.append(m)
    results = moves([(new_master, master_out), (new_one, one_out), (new_two, two_out)], left, PIECES)
    for copy in results:
        copy.start()
    parts = thirds(jnp.concatenate(updated, axis=1))
    picked = sum(dot(new, part, ((0,), (0,))) for part in reversed(parts))
    for f in range(rows):
        for p in range(slots):
            send[pl.ds(f * slots + p, owners, stride=rows * slots), :] = picked[
                p * owners : (p + 1) * owners, f * LANES : (f + 1) * LANES
            ]
    sent = moves(split(send, send_out), left)
    for copy in sent:
        copy.start()
    for copy in results + sent:
        copy.wait()


VMEM = pl.BlockSpec(memory_space=pltpu.VMEM)
SMEM = pl.BlockSpec(memory_space=pltpu.SMEM)
ANY = pl.BlockSpec(memory_space=pl.ANY)
SOME = 24 * 1024 * 1024
MUCH = 52 * 1024 * 1024
MOST = 60 * 1024 * 1024


def kernel(body, out_shape, in_specs, name, flops=0, limit=SOME, spec=VMEM, scratch=()):
    alone = not isinstance(out_shape, tuple)
    return pl.pallas_call(
        body,
        out_shape=out_shape,
        in_specs=in_specs,
        out_specs=spec if alone else (spec,) * len(out_shape),
        scratch_shapes=scratch,
        compiler_params=pltpu.CompilerParams(vmem_limit_bytes=limit),
        cost_estimate=pl.CostEstimate(flops=flops, bytes_accessed=4 << 20, transcendentals=0),
        name=name,
    )


def local(
    activations,
    out_grads,
    counts,
    slot_weights,
    master,
    moment_one,
    moment_two,
    old_table,
    new_table,
):
    f32 = jnp.float32
    dp = ("half", "slot")
    n = lax.axis_size("half") * lax.axis_size("slot")
    owners = lax.axis_size("ep")
    me = lax.axis_index("half") * lax.axis_size("slot") + lax.axis_index("slot")
    slots, tokens, ff = activations.shape
    experts, rows, lanes = master.shape
    width = ff + slots * lanes

    def shape(*dims):
        return jax.ShapeDtypeStruct(dims, f32)

    def scalar(x):
        return x.astype(jnp.int32).reshape(1)

    def exchange(x, axes):
        return lax.all_to_all(x, axes, split_axis=0, concat_axis=0, tiled=True)

    place = scalar(me)
    limits = counts[:, 0]
    packet = shape(tokens, width)
    work = 6 * slots * tokens * n * ff * lanes

    packed = kernel(pack_kernel, shape(n, tokens, width), [SMEM, VMEM, VMEM], "pack", limit=MOST)(
        limits, activations, out_grads
    )
    came = exchange(packed, dp)
    column_grad = kernel(grad_kernel, shape(slots * ff, lanes), [VMEM], "slot_grads", flops=work)(came)
    arrived = exchange(column_grad.reshape(slots * owners, 1, rows * lanes), ("slot", "ep"))

    given = kernel(swap_kernel, shape(ff, lanes), [ANY, SMEM, VMEM], "swap")(
        column_grad, scalar(lax.axis_index("slot")), slot_weights
    )
    other = lax.ppermute(given, "slot", [(0, 1), (1, 0)])
    plane = shape(rows, experts, lanes)
    flat = shape(slots * rows * owners, lanes)
    flip = lambda x: jnp.transpose(x, (1, 0, 2))
    new_master, new_one, new_two, send = kernel(
        adamw_kernel,
        (plane, plane, plane, flat),
        [ANY] * 7,
        "adamw",
        flops=work,
        limit=MUCH,
        spec=ANY,
        scratch=[pltpu.VMEM(flat.shape, f32)]
        + [pltpu.VMEM((1, slots * owners), jnp.int32)] * 2
        + [pltpu.VMEM(plane.shape, f32)] * 6
        + [pltpu.VMEM(flat.shape, f32)]
        + [pltpu.SemaphoreType.DMA((PIECES + 5,))] * 2,
    )(
        other,
        arrived.reshape(flat.shape),
        old_table.T,
        new_table.T,
        flip(master),
        flip(moment_one),
        flip(moment_two),
    )
    placed = exchange(send.reshape(owners, 1, slots * rows * lanes), "ep")
    parts = kernel(
        product_kernel,
        (packet,) * n,
        [ANY, SMEM, VMEM, VMEM, VMEM],
        "products",
        flops=2 * work,
        scratch=[pltpu.VMEM((n * tokens, width), f32)],
    )(send, place, slot_weights, other, came)

    back = [parts[0]] + [
        lax.ppermute(parts[k], dp, [(i, (i + k) % n) for i in range(n)]) for k in range(1, n)
    ]
    outputs, input_grads = kernel(
        combine_kernel,
        (shape(*out_grads.shape), shape(*activations.shape)),
        [SMEM, SMEM] + [VMEM] * n,
        "combine",
        scratch=[pltpu.VMEM((n, tokens, width), f32)],
    )(place, limits, *back)
    new_slots = kernel(place_kernel, shape(*slot_weights.shape), [VMEM], "new_slots")(
        placed.reshape(ff * slots, lanes)
    )
    return (outputs, input_grads, flip(new_master), flip(new_one), flip(new_two), new_slots)


def solution(mesh):
    ep, dp = mesh.devices.shape
    split = Mesh(mesh.devices.reshape(ep, dp // 2, 2), ("ep", "half", "slot"))
    both = ("half", "slot")
    in_specs = (
        P("ep", both, None),
        P("ep", both, None),
        P("ep", both),
        P("ep", None, both),
        P(None, "ep", both),
        P(None, "ep", both),
        P(None, "ep", both),
        P(),
        P(),
    )
    out_specs = (
        P("ep", both, None),
        P("ep", both, None),
        P(None, "ep", both),
        P(None, "ep", both),
        P(None, "ep", both),
        P("ep", None, both),
    )
    return jax.shard_map(local, mesh=split, in_specs=in_specs, out_specs=out_specs, check_vma=False)
```

```python
import jax
import jax.numpy as jnp
from jax import lax
from jax.experimental import pallas as pl
from jax.experimental.pallas import tpu as pltpu
from jax.sharding import Mesh, PartitionSpec as P

STEP = 100


beta_one = 0.9
beta_two = 0.999
learn_rate = 0.02
epsilon = 1e-08
decay_rate = 0.1

LANES = 128
PIECES = 4


def halves(x):
    high = x.astype(jnp.bfloat16)
    low = (x - high.astype(jnp.float32)).astype(jnp.bfloat16)
    return high, low


def thirds(x):
    high = x.astype(jnp.bfloat16)
    rest = x - high.astype(jnp.float32)
    middle = rest.astype(jnp.bfloat16)
    low = (rest - middle.astype(jnp.float32)).astype(jnp.bfloat16)
    return high, middle, low


def dot(a, b, dims):
    return lax.dot_general(a, b, (dims, ((), ())), preferred_element_type=jnp.float32)


def dot_split(a, b, dims):
    (ah, al), (bh, bl) = a, b
    return dot(ah, bh, dims) + (dot(ah, bl, dims) + dot(al, bh, dims))


def pack_kernel(counts, acts, grads, out):
    slots, rows, ff = acts.shape
    half = grads.shape[2] // slots
    for s in range(slots):
        live = lax.broadcasted_iota(jnp.int32, (rows, 1), 0) < counts[s]
        for b in range(slots):
            out[slots * b + s, :, :ff] = acts[s]
            out[slots * b + s, :, ff:] = jnp.where(live, grads[s, :, b * half : (b + 1) * half], 0.0)


def rows_of(came, ff):
    n, rows, width = came.shape
    a = came[:, :, :ff].reshape(n * rows, ff)
    g = came[:, :, ff:].reshape(n * rows, width - ff)
    return halves(a), halves(g)


def grad_kernel(came, out):
    ff = out.shape[0] // 2
    a, g = rows_of(came, ff)
    grad = dot_split(a, g, ((0,), (0,)))
    out[:ff] = grad[:, :LANES]
    out[ff:] = grad[:, LANES:]


def swap_kernel(after, slot, weights, out):
    out[...] = weights[1 - slot[0]]


def product_kernel(place, weights, other, came, *refs):
    outs, whole = refs[:-1], refs[-1]
    n, rows, _ = came.shape
    ff = weights.shape[1]
    slot = lax.rem(place[0], 2)
    mine, theirs = weights[slot], other[...]
    first = slot == 0
    w = halves(jnp.concatenate([jnp.where(first, mine, theirs), jnp.where(first, theirs, mine)], axis=1))
    a, g = rows_of(came, ff)
    whole[:, ff:] = dot_split(a, w, ((1,), (0,)))
    whole[:, :ff] = dot_split(g, w, ((1,), (1,)))
    for k, out in enumerate(outs):
        owner = lax.rem(place[0] + k, n)
        out[...] = whole[pl.ds(pl.multiple_of(owner * rows, rows), rows), :]


def combine_kernel(place, counts, *refs):
    parts, outputs, input_grads, whole = refs[:-3], refs[-3], refs[-2], refs[-1]
    n = len(parts)
    slots, rows, ff = input_grads.shape
    half = outputs.shape[2] // slots
    for k in range(n):
        whole[lax.rem(place[0] + n - k, n)] = parts[k][...]
    for s in range(slots):
        live = lax.broadcasted_iota(jnp.int32, (rows, 1), 0) < counts[s]
        input_grads[s] = whole[s, :, :ff] + whole[slots + s, :, :ff]
        for b in range(slots):
            outputs[s, :, b * half : (b + 1) * half] = jnp.where(live, whole[slots * b + s, :, ff:], 0.0)


def place_kernel(rows, out):
    slots, ff, _ = out.shape
    for s in range(slots):
        out[s] = rows[pl.ds(s, ff, stride=slots), :]


def adamw_kernel(after, arrived_in, old_in, new_in, master_in, one_in, two_in,
                 master_out, one_out, two_out, send_out,
                 arrived, old_table, new_table, master, moment_one, moment_two, new_master, new_one, new_two, send, landed, left):
    def moves(pairs, signals, first=0):
        return [pltpu.make_async_copy(a, b, signals.at[first + i]) for i, (a, b) in enumerate(pairs)]

    def split(a, b):
        part = a.shape[0] // PIECES
        return [(a.at[pl.ds(i * part, part)], b.at[pl.ds(i * part, part)]) for i in range(PIECES)]

    tables = moves([(old_in, old_table), (new_in, new_table)], landed, PIECES + 3)
    early = moves(split(arrived_in, arrived), landed)
    later = moves([(master_in, master), (one_in, moment_one), (two_in, moment_two)], landed, PIECES)
    for copy in tables + early + later:
        copy.start()
    rows, experts, _ = master.shape
    total = old_table.shape[1]
    slots = 2
    owners = total // slots
    source = lax.broadcasted_iota(jnp.int32, (total, total), 0)
    target = lax.broadcasted_iota(jnp.int32, (total, total), 1)
    wanted = slots * lax.rem(target, owners) + target // owners
    order = (source == wanted).astype(jnp.float32).astype(jnp.bfloat16)
    ids = lax.broadcasted_iota(jnp.int32, (experts, total), 0)

    def onehot(table):
        named = jnp.broadcast_to(table[...].astype(jnp.float32), (8, total)).astype(jnp.bfloat16)
        named = dot(named, order, ((1,), (0,)))[:1].astype(jnp.int32)
        return (ids == named).astype(jnp.float32).astype(jnp.bfloat16)

    for copy in tables:
        copy.wait()
    old = onehot(old_table)
    new = onehot(new_table)
    for copy in early:
        copy.wait()
    got = jnp.concatenate([arrived[pl.ds(f, total, stride=rows), :] for f in range(rows)], axis=1)
    grad = sum(dot(old, part, ((1,), (0,))) for part in reversed(thirds(got)))
    for copy in later:
        copy.wait()
    updated = []
    for f in range(rows):
        g = grad[:, f * LANES : (f + 1) * LANES]
        first = beta_one * moment_one[f] + (1.0 - beta_one) * g
        second = beta_two * moment_two[f] + (1.0 - beta_two) * g * g
        new_one[f] = first
        new_two[f] = second
        first_hat = first / (1.0 - beta_one**STEP)
        second_hat = second / (1.0 - beta_two**STEP)
        m = master[f]
        m = m - learn_rate * (first_hat / (jnp.sqrt(second_hat) + epsilon) + decay_rate * m)
        new_master[f] = m
        updated.append(m)
    results = moves([(new_master, master_out), (new_one, one_out), (new_two, two_out)], left, PIECES)
    for copy in results:
        copy.start()
    parts = thirds(jnp.concatenate(updated, axis=1))
    picked = sum(dot(new, part, ((0,), (0,))) for part in reversed(parts))
    for f in range(rows):
        for p in range(slots):
            send[pl.ds(f * slots + p, owners, stride=rows * slots), :] = picked[
                p * owners : (p + 1) * owners, f * LANES : (f + 1) * LANES
            ]
    sent = moves(split(send, send_out), left)
    for copy in sent:
        copy.start()
    for copy in results + sent:
        copy.wait()


VMEM = pl.BlockSpec(memory_space=pltpu.VMEM)
SMEM = pl.BlockSpec(memory_space=pltpu.SMEM)
ANY = pl.BlockSpec(memory_space=pl.ANY)
SOME = 24 * 1024 * 1024
MOST = 60 * 1024 * 1024


def kernel(body, out_shape, in_specs, name, flops=0, limit=SOME, spec=VMEM, scratch=()):
    alone = not isinstance(out_shape, tuple)
    return pl.pallas_call(
        body,
        out_shape=out_shape,
        in_specs=in_specs,
        out_specs=spec if alone else (spec,) * len(out_shape),
        scratch_shapes=scratch,
        compiler_params=pltpu.CompilerParams(vmem_limit_bytes=limit),
        cost_estimate=pl.CostEstimate(flops=flops, bytes_accessed=4 << 20, transcendentals=0),
        name=name,
    )


def local(
    activations,
    out_grads,
    counts,
    slot_weights,
    master,
    moment_one,
    moment_two,
    old_table,
    new_table,
):
    f32 = jnp.float32
    dp = ("half", "slot")
    n = lax.axis_size("half") * lax.axis_size("slot")
    owners = lax.axis_size("ep")
    me = lax.axis_index("half") * lax.axis_size("slot") + lax.axis_index("slot")
    slots, tokens, ff = activations.shape
    experts, rows, lanes = master.shape
    width = ff + slots * lanes

    def shape(*dims):
        return jax.ShapeDtypeStruct(dims, f32)

    def scalar(x):
        return x.astype(jnp.int32).reshape(1)

    def exchange(x, axes):
        return lax.all_to_all(x, axes, split_axis=0, concat_axis=0, tiled=True)

    place = scalar(me)
    limits = counts[:, 0]
    packet = shape(tokens, width)
    work = 6 * slots * tokens * n * ff * lanes

    packed = kernel(pack_kernel, shape(n, tokens, width), [SMEM, VMEM, VMEM], "pack", limit=MOST)(
        limits, activations, out_grads
    )
    came = exchange(packed, dp)
    column_grad = kernel(grad_kernel, shape(slots * ff, lanes), [VMEM], "slot_grads", flops=work)(came)
    arrived = exchange(column_grad.reshape(slots * owners, 1, rows * lanes), ("slot", "ep"))

    given = kernel(swap_kernel, shape(ff, lanes), [ANY, SMEM, VMEM], "swap")(
        column_grad, scalar(lax.axis_index("slot")), slot_weights
    )
    other = lax.ppermute(given, "slot", [(0, 1), (1, 0)])
    parts = kernel(
        product_kernel,
        (packet,) * n,
        [SMEM, VMEM, VMEM, VMEM],
        "products",
        flops=2 * work,
        scratch=[pltpu.VMEM((n * tokens, width), f32)],
    )(place, slot_weights, other, came)

    plane = shape(rows, experts, lanes)
    flat = shape(slots * rows * owners, lanes)
    flip = lambda x: jnp.transpose(x, (1, 0, 2))
    new_master, new_one, new_two, send = kernel(
        adamw_kernel,
        (plane, plane, plane, flat),
        [ANY] * 7,
        "adamw",
        flops=work,
        limit=MOST,
        spec=ANY,
        scratch=[pltpu.VMEM(flat.shape, f32)]
        + [pltpu.VMEM((1, slots * owners), jnp.int32)] * 2
        + [pltpu.VMEM(plane.shape, f32)] * 6
        + [pltpu.VMEM(flat.shape, f32)]
        + [pltpu.SemaphoreType.DMA((PIECES + 5,))] * 2,
    )(
        parts[0],
        arrived.reshape(flat.shape),
        old_table.T,
        new_table.T,
        flip(master),
        flip(moment_one),
        flip(moment_two),
    )
    placed = exchange(send.reshape(owners, 1, slots * rows * lanes), "ep")
    back = [parts[0]] + [
        lax.ppermute(parts[k], dp, [(i, (i + k) % n) for i in range(n)]) for k in range(1, n)
    ]
    outputs, input_grads = kernel(
        combine_kernel,
        (shape(*out_grads.shape), shape(*activations.shape)),
        [SMEM, SMEM] + [VMEM] * n,
        "combine",
        scratch=[pltpu.VMEM((n, tokens, width), f32)],
    )(place, limits, *back)
    new_slots = kernel(place_kernel, shape(*slot_weights.shape), [VMEM], "new_slots")(
        placed.reshape(ff * slots, lanes)
    )
    return (outputs, input_grads, flip(new_master), flip(new_one), flip(new_two), new_slots)


def solution(mesh):
    ep, dp = mesh.devices.shape
    split = Mesh(mesh.devices.reshape(ep, dp // 2, 2), ("ep", "half", "slot"))
    both = ("half", "slot")
    in_specs = (
        P("ep", both, None),
        P("ep", both, None),
        P("ep", both),
        P("ep", None, both),
        P(None, "ep", both),
        P(None, "ep", both),
        P(None, "ep", both),
        P(),
        P(),
    )
    out_specs = (
        P("ep", both, None),
        P("ep", both, None),
        P(None, "ep", both),
        P(None, "ep", both),
        P(None, "ep", both),
        P("ep", None, both),
    )
    return jax.shard_map(local, mesh=split, in_specs=in_specs, out_specs=out_specs, check_vma=False)
```

```python
import jax
import jax.numpy as jnp
from jax import lax
from jax.experimental import pallas as pl
from jax.experimental.pallas import tpu as pltpu
from jax.sharding import Mesh, PartitionSpec as P

STEP = 100


beta_one = 0.9
beta_two = 0.999
learn_rate = 0.02
epsilon = 1e-08
decay_rate = 0.1

LANES = 128
PIECES = 4


def halves(x):
    high = x.astype(jnp.bfloat16)
    low = (x - high.astype(jnp.float32)).astype(jnp.bfloat16)
    return high, low


def thirds(x):
    high = x.astype(jnp.bfloat16)
    rest = x - high.astype(jnp.float32)
    middle = rest.astype(jnp.bfloat16)
    low = (rest - middle.astype(jnp.float32)).astype(jnp.bfloat16)
    return high, middle, low


def dot(a, b, dims):
    return lax.dot_general(a, b, (dims, ((), ())), preferred_element_type=jnp.float32)


def dot_split(a, b, dims):
    (ah, al), (bh, bl) = a, b
    return dot(ah, bh, dims) + (dot(ah, bl, dims) + dot(al, bh, dims))


def pack_kernel(counts, acts, grads, out):
    slots, rows, ff = acts.shape
    half = grads.shape[2] // slots
    for s in range(slots):
        live = lax.broadcasted_iota(jnp.int32, (rows, 1), 0) < counts[s]
        for b in range(slots):
            out[slots * b + s, :, :ff] = acts[s]
            out[slots * b + s, :, ff:] = jnp.where(live, grads[s, :, b * half : (b + 1) * half], 0.0)


def rows_of(came, ff):
    n, rows, width = came.shape
    a = came[:, :, :ff].reshape(n * rows, ff)
    g = came[:, :, ff:].reshape(n * rows, width - ff)
    return halves(a), halves(g)


def grad_kernel(came, out):
    ff = out.shape[0] // 2
    a, g = rows_of(came, ff)
    grad = dot_split(a, g, ((0,), (0,)))
    out[:ff] = grad[:, :LANES]
    out[ff:] = grad[:, LANES:]


def swap_kernel(after, slot, weights, out):
    out[...] = weights[1 - slot[0]]


def product_kernel(place, weights, other, came, *refs):
    outs, done, whole = refs[:-2], refs[-2], refs[-1]
    done[...] = jnp.zeros_like(done)
    n, rows, _ = came.shape
    ff = weights.shape[1]
    slot = lax.rem(place[0], 2)
    mine, theirs = weights[slot], other[...]
    first = slot == 0
    w = halves(jnp.concatenate([jnp.where(first, mine, theirs), jnp.where(first, theirs, mine)], axis=1))
    a, g = rows_of(came, ff)
    whole[:, ff:] = dot_split(a, w, ((1,), (0,)))
    whole[:, :ff] = dot_split(g, w, ((1,), (1,)))
    for k, out in enumerate(outs):
        owner = lax.rem(place[0] + k, n)
        out[...] = whole[pl.ds(pl.multiple_of(owner * rows, rows), rows), :]


def combine_kernel(place, counts, *refs):
    parts, outputs, input_grads, whole = refs[:-3], refs[-3], refs[-2], refs[-1]
    n = len(parts)
    slots, rows, ff = input_grads.shape
    half = outputs.shape[2] // slots
    for k in range(n):
        whole[lax.rem(place[0] + n - k, n)] = parts[k][...]
    for s in range(slots):
        live = lax.broadcasted_iota(jnp.int32, (rows, 1), 0) < counts[s]
        input_grads[s] = whole[s, :, :ff] + whole[slots + s, :, :ff]
        for b in range(slots):
            outputs[s, :, b * half : (b + 1) * half] = jnp.where(live, whole[slots * b + s, :, ff:], 0.0)


def place_kernel(rows, out):
    slots, ff, _ = out.shape
    for s in range(slots):
        out[s] = rows[pl.ds(s, ff, stride=slots), :]


def adamw_kernel(after, arrived_in, old_in, new_in, master_in, one_in, two_in,
                 master_out, one_out, two_out, send_out,
                 arrived, old_table, new_table, master, moment_one, moment_two, new_master, new_one, new_two, send, landed, left):
    def moves(pairs, signals, first=0):
        return [pltpu.make_async_copy(a, b, signals.at[first + i]) for i, (a, b) in enumerate(pairs)]

    def split(a, b):
        part = a.shape[0] // PIECES
        return [(a.at[pl.ds(i * part, part)], b.at[pl.ds(i * part, part)]) for i in range(PIECES)]

    tables = moves([(old_in, old_table), (new_in, new_table)], landed, PIECES + 3)
    early = moves(split(arrived_in, arrived), landed)
    later = moves([(master_in, master), (one_in, moment_one), (two_in, moment_two)], landed, PIECES)
    for copy in tables + early + later:
        copy.start()
    rows, experts, _ = master.shape
    total = old_table.shape[1]
    slots = 2
    owners = total // slots
    source = lax.broadcasted_iota(jnp.int32, (total, total), 0)
    target = lax.broadcasted_iota(jnp.int32, (total, total), 1)
    wanted = slots * lax.rem(target, owners) + target // owners
    order = (source == wanted).astype(jnp.float32).astype(jnp.bfloat16)
    ids = lax.broadcasted_iota(jnp.int32, (experts, total), 0)

    def onehot(table):
        named = jnp.broadcast_to(table[...].astype(jnp.float32), (8, total)).astype(jnp.bfloat16)
        named = dot(named, order, ((1,), (0,)))[:1].astype(jnp.int32)
        return (ids == named).astype(jnp.float32).astype(jnp.bfloat16)

    for copy in tables:
        copy.wait()
    old = onehot(old_table)
    new = onehot(new_table)
    for copy in early:
        copy.wait()
    got = jnp.concatenate([arrived[pl.ds(f, total, stride=rows), :] for f in range(rows)], axis=1)
    grad = sum(dot(old, part, ((1,), (0,))) for part in reversed(thirds(got)))
    for copy in later:
        copy.wait()
    updated = []
    for f in range(rows):
        g = grad[:, f * LANES : (f + 1) * LANES]
        first = beta_one * moment_one[f] + (1.0 - beta_one) * g
        second = beta_two * moment_two[f] + (1.0 - beta_two) * g * g
        new_one[f] = first
        new_two[f] = second
        first_hat = first / (1.0 - beta_one**STEP)
        second_hat = second / (1.0 - beta_two**STEP)
        m = master[f]
        m = m - learn_rate * (first_hat / (jnp.sqrt(second_hat) + epsilon) + decay_rate * m)
        new_master[f] = m
        updated.append(m)
    results = moves([(new_master, master_out), (new_one, one_out), (new_two, two_out)], left, PIECES)
    for copy in results:
        copy.start()
    parts = thirds(jnp.concatenate(updated, axis=1))
    picked = sum(dot(new, part, ((0,), (0,))) for part in reversed(parts))
    for f in range(rows):
        for p in range(slots):
            send[pl.ds(f * slots + p, owners, stride=rows * slots), :] = picked[
                p * owners : (p + 1) * owners, f * LANES : (f + 1) * LANES
            ]
    sent = moves(split(send, send_out), left)
    for copy in sent:
        copy.start()
    for copy in results + sent:
        copy.wait()


VMEM = pl.BlockSpec(memory_space=pltpu.VMEM)
SMEM = pl.BlockSpec(memory_space=pltpu.SMEM)
ANY = pl.BlockSpec(memory_space=pl.ANY)
SOME = 24 * 1024 * 1024
MOST = 60 * 1024 * 1024


def kernel(body, out_shape, in_specs, name, flops=0, limit=SOME, spec=VMEM, scratch=()):
    alone = not isinstance(out_shape, tuple)
    return pl.pallas_call(
        body,
        out_shape=out_shape,
        in_specs=in_specs,
        out_specs=spec if alone else (spec,) * len(out_shape),
        scratch_shapes=scratch,
        compiler_params=pltpu.CompilerParams(vmem_limit_bytes=limit),
        cost_estimate=pl.CostEstimate(flops=flops, bytes_accessed=4 << 20, transcendentals=0),
        name=name,
    )


def local(
    activations,
    out_grads,
    counts,
    slot_weights,
    master,
    moment_one,
    moment_two,
    old_table,
    new_table,
):
    f32 = jnp.float32
    dp = ("half", "slot")
    n = lax.axis_size("half") * lax.axis_size("slot")
    owners = lax.axis_size("ep")
    me = lax.axis_index("half") * lax.axis_size("slot") + lax.axis_index("slot")
    slots, tokens, ff = activations.shape
    experts, rows, lanes = master.shape
    width = ff + slots * lanes

    def shape(*dims):
        return jax.ShapeDtypeStruct(dims, f32)

    def scalar(x):
        return x.astype(jnp.int32).reshape(1)

    def exchange(x, axes):
        return lax.all_to_all(x, axes, split_axis=0, concat_axis=0, tiled=True)

    place = scalar(me)
    limits = counts[:, 0]
    packet = shape(tokens, width)
    work = 6 * slots * tokens * n * ff * lanes

    packed = kernel(pack_kernel, shape(n, tokens, width), [SMEM, VMEM, VMEM], "pack", limit=MOST)(
        limits, activations, out_grads
    )
    came = exchange(packed, dp)
    column_grad = kernel(grad_kernel, shape(slots * ff, lanes), [VMEM], "slot_grads", flops=work)(came)
    arrived = exchange(column_grad.reshape(slots * owners, 1, rows * lanes), ("slot", "ep"))

    given = kernel(swap_kernel, shape(ff, lanes), [ANY, SMEM, VMEM], "swap")(
        column_grad, scalar(lax.axis_index("slot")), slot_weights
    )
    other = lax.ppermute(given, "slot", [(0, 1), (1, 0)])
    *parts, done = kernel(
        product_kernel,
        (packet,) * n + (shape(8, lanes),),
        [SMEM, VMEM, VMEM, VMEM],
        "products",
        flops=2 * work,
        scratch=[pltpu.VMEM((n * tokens, width), f32)],
    )(place, slot_weights, other, came)

    plane = shape(rows, experts, lanes)
    flat = shape(slots * rows * owners, lanes)
    flip = lambda x: jnp.transpose(x, (1, 0, 2))
    new_master, new_one, new_two, send = kernel(
        adamw_kernel,
        (plane, plane, plane, flat),
        [ANY] * 7,
        "adamw",
        flops=work,
        limit=MOST,
        spec=ANY,
        scratch=[pltpu.VMEM(flat.shape, f32)]
        + [pltpu.VMEM((1, slots * owners), jnp.int32)] * 2
        + [pltpu.VMEM(plane.shape, f32)] * 6
        + [pltpu.VMEM(flat.shape, f32)]
        + [pltpu.SemaphoreType.DMA((PIECES + 5,))] * 2,
    )(
        done,
        arrived.reshape(flat.shape),
        old_table.T,
        new_table.T,
        flip(master),
        flip(moment_one),
        flip(moment_two),
    )
    placed = exchange(send.reshape(owners, 1, slots * rows * lanes), "ep")
    back = [parts[0]] + [
        lax.ppermute(parts[k], dp, [(i, (i + k) % n) for i in range(n)]) for k in range(1, n)
    ]
    outputs, input_grads = kernel(
        combine_kernel,
        (shape(*out_grads.shape), shape(*activations.shape)),
        [SMEM, SMEM] + [VMEM] * n,
        "combine",
        scratch=[pltpu.VMEM((n, tokens, width), f32)],
    )(place, limits, *back)
    new_slots = kernel(place_kernel, shape(*slot_weights.shape), [VMEM], "new_slots")(
        placed.reshape(ff * slots, lanes)
    )
    return (outputs, input_grads, flip(new_master), flip(new_one), flip(new_two), new_slots)


def solution(mesh):
    ep, dp = mesh.devices.shape
    split = Mesh(mesh.devices.reshape(ep, dp // 2, 2), ("ep", "half", "slot"))
    both = ("half", "slot")
    in_specs = (
        P("ep", both, None),
        P("ep", both, None),
        P("ep", both),
        P("ep", None, both),
        P(None, "ep", both),
        P(None, "ep", both),
        P(None, "ep", both),
        P(),
        P(),
    )
    out_specs = (
        P("ep", both, None),
        P("ep", both, None),
        P(None, "ep", both),
        P(None, "ep", both),
        P(None, "ep", both),
        P("ep", None, both),
    )
    return jax.shard_map(local, mesh=split, in_specs=in_specs, out_specs=out_specs, check_vma=False)
```
